128 devices in a mesh: row: 16 (over y, x), col: 8 (over z, core).
Axes of the slice: x: 4, y: 4, z: 4, core: 2. Of those that a mesh axis runs over, the one named last changes fastest.
Arguments:
- owned_rows: bfloat16 [3072, 8192], P(('row', 'col')), may hold values from -6 to 6
- suffix_lengths: int32 [128], replicated, may hold values from 1 to 24, 1024 in all
- owner_map: int32 [128], replicated, may hold values from 0 to 127, each once
- prefix_lengths: int32 [128], replicated, may hold values from 0 to 4095
- gate_weight: bfloat16 [8192, 29568], P('row', 'col'), may hold values from -0.0625 to 0.0625
- up_weight: bfloat16 [8192, 29568], P('row', 'col'), may hold values from -0.0625 to 0.0625
- down_weight: bfloat16 [29568, 8192], P('col', 'row'), may hold values from -0.03125 to 0.03125
Outputs:
- mixed: bfloat16 [1024, 8192], P('col', 'row')
The draws below stay inside these ranges and needn't reach their ends.
Inputs may be any that keep to these rules, and one draw needn't show every extreme that they name: `suffix_lengths`: the lengths add up to 1024; the largest is exactly 24. `owner_map`: each device owns one request; request r's suffix rows fill, in order, the first suffix_lengths[r] of the 24 slots of its owner in owned_rows, and the other slots are not used.
All inputs are finite; a program needn't handle non-finite values.
Results may differ from the reference program's by a relative error of at most 0.0049.
Values may be sent and summed in bfloat16 or wider, within the bound.
No kernel may reach another device: no remote copies, remote signals or barrier semaphores. Data moves between devices by JAX's collectives and lax.ppermute only.
A program may use at most 128 MiB of HBM per device.

```python
import math
import jax
import jax.numpy as jnp
import numpy as np

D = 8192
FF = 29568
PREFIX_MAX = 4096
REQS = 128
TOKENS = 1024
MOST = 24


def draw_prefix_lengths(key, part):
    base_key, pick_key = jax.random.split(jax.random.fold_in(key, 7))
    drawn_lengths = jax.random.randint(base_key, (REQS,), 0, PREFIX_MAX, dtype=jnp.int32)
    chosen = jax.random.permutation(pick_key, REQS)
    drawn_lengths = drawn_lengths.at[chosen[0]].set(PREFIX_MAX - 1)
    return drawn_lengths.at[chosen[1]].set(0)


def level_of(key, extent, pieces, least, largest):
    factor_of = 1.0
    for dim, parts in pieces:
        steps = jax.random.uniform(jax.random.fold_in(jax.random.fold_in(key, 6), dim), (parts,), jnp.float32, least / len(pieces), largest / len(pieces))
        factor_of = factor_of * jnp.repeat(jnp.exp(steps), extent[dim] // parts).reshape((-1,) + (1,) * (len(extent) - 1 - dim))
    return factor_of


def split_up(number_of, total, bound, slope):
    portions = [(1 << 20) // math.isqrt(rank ** slope) + 1 for rank in range(2, number_of + 1)]
    surplus, counts = total - bound - (number_of - 1), [1] * (number_of - 1)
    while surplus > 0:
        movable = [i for i in range(number_of - 1) if counts[i] < bound]
        mass, left = sum([portions[i] for i in movable]), surplus
        for i in movable:
            more = min(bound - counts[i], max(1, left * portions[i] // mass), surplus)
            counts[i] = counts[i] + more
            surplus = surplus - more
    return np.array([bound] + counts)


def uneven_parts(rng, count, total, limit, skew):
    if count == 2:
        one = jax.random.randint(rng, (), max(1, total - limit), min(limit, total - 1) + 1)
        return jnp.stack([one, total - one])
    sizes = jnp.asarray(split_up(count, total, limit, skew), jnp.int32)
    couples = (count - 1) // 2
    donor, sink = sizes[1:1 + 2 * couples:2], sizes[2:2 + 2 * couples:2]
    room = jnp.minimum(donor - 1, limit - sink)
    moved = jax.random.randint(jax.random.fold_in(rng, 1), (couples,), 0, 1 << 20) % (room + 1)
    sizes = sizes.at[1:1 + 2 * couples:2].set(donor - moved).at[2:2 + 2 * couples:2].set(sink + moved)
    return sizes[jax.random.permutation(jax.random.fold_in(rng, 2), count)]


def gaussian(key, shape, scale, most, pieces=(), held_as=jnp.bfloat16):
    array = scale * jax.random.normal(key, shape, jnp.float32)
    if pieces:
        array = array * level_of(key, shape, pieces, -0.22, 0.18)
    return jnp.clip(array, -most, most).astype(held_as)


def setup_inputs(seed: int = 0) -> dict:
    arg_keys = jax.random.split(jax.random.key(seed), 8)
    return {
        "owned_rows": gaussian(arg_keys[0], (REQS * MOST, D), 1.0, 6.0, ((0, 128),)),
        "suffix_lengths": uneven_parts(arg_keys[1], REQS, TOKENS, MOST, 2).astype(jnp.int32),
        "owner_map": jax.random.permutation(arg_keys[2], REQS).astype(jnp.int32),
        "prefix_lengths": draw_prefix_lengths(jax.random.fold_in(arg_keys[7], 71), 0),
        "gate_weight": gaussian(arg_keys[4], (D, FF), D ** -0.5, 0.0625, ((0, 16), (1, 8))),
        "up_weight": gaussian(arg_keys[5], (D, FF), D ** -0.5, 0.0625, ((0, 16), (1, 8))),
        "down_weight": gaussian(arg_keys[6], (FF, D), FF ** -0.5, 0.03125, ((0, 8), (1, 16))),
    }


def source_rows(suffix_lengths, owner_map, prefix_lengths, row_count, slot_size):
    request_ids = jnp.arange(suffix_lengths.shape[0], dtype=jnp.int32)
    longer = prefix_lengths[None, :] > prefix_lengths[:, None]
    earlier = (prefix_lengths[None, :] == prefix_lengths[:, None]) & (request_ids[None, :] < request_ids[:, None])
    starts = jnp.sum(jnp.where(longer | earlier, suffix_lengths[None, :], 0), axis=1).astype(jnp.int32)
    positions = jnp.arange(row_count, dtype=jnp.int32)
    ends = (starts + suffix_lengths).astype(jnp.int32)
    inside = (positions[:, None] >= starts[None, :]) & (positions[:, None] < ends[None, :])
    offsets = (owner_map * slot_size - starts).astype(jnp.int32)
    shifted = jnp.sum(jnp.where(inside, offsets[None, :], 0), axis=1).astype(jnp.int32)
    return (positions + shifted).astype(jnp.int32)


def reference(owned_rows, suffix_lengths, owner_map, prefix_lengths, gate_weight, up_weight, down_weight):
    source = source_rows(suffix_lengths, owner_map, prefix_lengths, TOKENS, MOST)
    suffix_rows = jnp.take(owned_rows, source, axis=0)
    gate_sum = jnp.dot(suffix_rows, gate_weight, preferred_element_type=jnp.float32)
    up_sum = jnp.dot(suffix_rows, up_weight, preferred_element_type=jnp.float32)
    hidden = (jax.nn.silu(gate_sum) * up_sum).astype(jnp.bfloat16)
    return jnp.dot(hidden, down_weight, preferred_element_type=jnp.float32).astype(jnp.bfloat16)
```

```python
import jax
import jax.numpy as jnp
from jax import lax
from jax.experimental import pallas as pl
from jax.experimental.pallas import tpu as pltpu
from jax.sharding import Mesh, PartitionSpec as P

SIDE = 4
CORES = 2
SUB = 232
BLOCK = 2 * SUB
HALF = SIDE * BLOCK
TOK_DEV = 8
BF16 = jnp.bfloat16
F32 = jnp.float32


def shift(value, axis, by, size=SIDE):
    return lax.ppermute(value, axis, [(i, (i + by) % size) for i in range(size)])


def around(value, axis):
    return [value] + [shift(value, axis, by) for by in range(1, SIDE)]


def exchange(value, axis):
    return lax.all_to_all(value, axis, split_axis=0, concat_axis=0, tiled=True)


def source_rows(suffix_lengths, owner_map, prefix_lengths, positions):
    request_ids = jnp.arange(suffix_lengths.shape[0], dtype=jnp.int32)
    longer = prefix_lengths[None, :] > prefix_lengths[:, None]
    earlier = (prefix_lengths[None, :] == prefix_lengths[:, None]) & (
        request_ids[None, :] < request_ids[:, None]
    )
    starts = jnp.sum(jnp.where(longer | earlier, suffix_lengths[None, :], 0), axis=1)
    ends = starts + suffix_lengths
    inside = (positions[:, None] >= starts[None, :]) & (positions[:, None] < ends[None, :])
    row, col = owner_map // (SIDE * CORES), owner_map % (SIDE * CORES)
    z_behind = (lax.axis_index("z") - col // CORES) % SIDE
    other_core = (lax.axis_index("core") + col) % CORES
    slot = ((other_core * SIDE + z_behind) * SIDE * SIDE + row) * 24
    shifted = jnp.sum(jnp.where(inside, (slot - starts)[None, :], 0), axis=1)
    return positions + shifted


def partial_kernel(order_ref, own_ref, other_ref, x0, x1, x2, x3, out_ref):
    def products(weight_ref):
        total = None
        for behind, rows in enumerate((x0, x1, x2, x3)):
            term = lax.dot_general(
                weight_ref[order_ref[behind], 0],
                rows[...],
                (((1,), (1,)), ((), ())),
                preferred_element_type=F32,
            )
            total = term if total is None else total + term
        out_ref[0] = total.astype(BF16)

    @pl.when(pl.program_id(0) == 0)
    def _():
        products(own_ref)

    @pl.when(pl.program_id(0) == 1)
    def _():
        products(other_ref)


def partial_products(order, own, other, rows):
    features = own.shape[-1]
    whole = pl.BlockSpec(rows[0].shape, lambda c, s, order: (0, 0))
    return pl.pallas_call(
        partial_kernel,
        grid_spec=pltpu.PrefetchScalarGridSpec(
            num_scalar_prefetch=1,
            grid=(2, 2),
            in_specs=[
                pl.BlockSpec((SIDE, 1, BLOCK, features), lambda c, s, order: (0, s * (1 - c) + c, 0, 0)),
                pl.BlockSpec((SIDE, 1, BLOCK, features), lambda c, s, order: (0, s * c, 0, 0)),
            ]
            + [whole] * SIDE,
            out_specs=pl.BlockSpec((1, BLOCK, rows[0].shape[0]), lambda c, s, order: (2 * c + s, 0, 0)),
        ),
        out_shape=jax.ShapeDtypeStruct((SIDE, BLOCK, rows[0].shape[0]), BF16),
    )(order, own, other, *rows)


def hidden_kernel(parts_ref, out_ref):
    total = parts_ref[0].astype(F32)
    for i in range(1, SIDE):
        total = total + parts_ref[i].astype(F32)
    gate, up = total[:SUB], total[SUB:]
    out_ref[...] = (gate / (1.0 + jnp.exp(-gate)) * up).astype(BF16)


def hidden_rows(parts):
    return pl.pallas_call(
        hidden_kernel,
        out_shape=jax.ShapeDtypeStruct((SUB, parts.shape[-1]), BF16),
    )(parts)


def down_kernel(*refs):
    out_ref, weights, hiddens = refs[-1], refs[:2], refs[2:-1]
    total = None
    for half in range(2):
        for behind in range(SIDE):
            hidden = hiddens[half * SIDE + behind]
            for i in range(SIDE):
                term = lax.dot_general(
                    hidden[i],
                    weights[half][behind, i],
                    (((0,), (0,)), ((), ())),
                    preferred_element_type=F32,
                )
                total = term if total is None else total + term
    out_ref[...] = total


def down_products(weights, hiddens):
    tokens, features = hiddens[0].shape[-1], weights[0].shape[-1]
    return pl.pallas_call(
        down_kernel,
        out_shape=jax.ShapeDtypeStruct((tokens, features), F32),
    )(*weights, *hiddens)


def on_device(
    owned_rows, suffix_lengths, owner_map, prefix_lengths, gate_weight, up_weight, down_weight
):
    slots = owned_rows.shape[0]
    features = gate_weight.shape[0]
    x, y = lax.axis_index("x"), lax.axis_index("y")
    core = lax.axis_index("core")
    behind = jnp.arange(SIDE, dtype=jnp.int32)
    x_order, y_order = (x - behind) % SIDE, (y - behind) % SIDE

    pad = ((0, 2 * HALF - gate_weight.shape[1]), (0, 0))
    gate, up = jnp.pad(gate_weight.T, pad), jnp.pad(up_weight.T, pad)

    def halves(weight):
        return weight.reshape(2, SIDE, 2, SUB, features)

    both = jnp.concatenate([halves(gate), halves(up)], axis=3)
    own_x, own_y = exchange(both[0], "x"), exchange(both[1], "y")
    other_x, other_y = shift(own_x, "core", 1, 2), shift(own_y, "core", 1, 2)

    down = jnp.pad(down_weight, pad).reshape(2, SIDE, 2, SUB, features)
    down = jnp.concatenate([down, shift(down, "core", 1, 2)], axis=2)
    down_x = jnp.take(jnp.take(down[0], x_order, axis=0), y_order, axis=1)
    down_y = jnp.take(jnp.take(down[1], y_order, axis=0), x_order, axis=1)

    blocks = owned_rows.reshape(slots, SIDE * SIDE, features).transpose(1, 0, 2)
    feature_rows = exchange(blocks, ("y", "x")).reshape(-1, features)
    near = jnp.concatenate(around(feature_rows, "z"), axis=0)
    every = jnp.concatenate([near, shift(near, "core", 1, 2)], axis=0)
    place = jnp.arange(TOK_DEV * suffix_lengths.shape[0] // CORES, dtype=jnp.int32)
    positions = (place // 128 * CORES + core) * 128 + place % 128
    source = source_rows(suffix_lengths, owner_map, prefix_lengths, positions)
    rows = every.at[source].get(mode="promise_in_bounds")

    part_x = partial_products(x_order, own_x, other_x, around(rows, "x"))
    part_y = partial_products(y_order, own_y, other_y, around(rows, "y"))
    hidden_x = hidden_rows(exchange(part_x, "y"))
    hidden_y = hidden_rows(exchange(part_y, "x"))

    all_x = around(jnp.stack(around(hidden_x, "y")), "x")
    all_y = around(jnp.stack(around(hidden_y, "x")), "y")
    partial_sums = down_products([down_x, down_y], all_x + all_y)
    parts = exchange(partial_sums.reshape(SIDE, -1, features), "z")
    return jnp.sum(parts, axis=0).astype(BF16)


def solution(mesh):
    torus = Mesh(mesh.devices.reshape(SIDE, SIDE, SIDE, CORES), ("y", "x", "z", "core"))
    row, col = ("y", "x"), ("z", "core")
    return jax.shard_map(
        on_device,
        mesh=torus,
        in_specs=(P(row + col, None), P(), P(), P(), P(row, col), P(row, col), P(col, row)),
        out_specs=P(col, row),
        check_vma=False,
    )
```

```python
import jax
import jax.numpy as jnp
from jax import lax
from jax.experimental import pallas as pl
from jax.experimental.pallas import tpu as pltpu
from jax.sharding import Mesh, PartitionSpec as P

SIDE = 4
CORES = 2
SUB = 232
BLOCK = 2 * SUB
HALF = SIDE * BLOCK
TOK_DEV = 8
BF16 = jnp.bfloat16
F32 = jnp.float32


def shift(value, axis, by, size=SIDE):
    return lax.ppermute(value, axis, [(i, (i + by) % size) for i in range(size)])


def around(value, axis):
    return [value] + [shift(value, axis, by) for by in range(1, SIDE)]


def exchange(value, axis):
    return lax.all_to_all(value, axis, split_axis=0, concat_axis=0, tiled=True)


def source_rows(suffix_lengths, owner_map, prefix_lengths, positions):
    request_ids = jnp.arange(suffix_lengths.shape[0], dtype=jnp.int32)
    longer = prefix_lengths[None, :] > prefix_lengths[:, None]
    earlier = (prefix_lengths[None, :] == prefix_lengths[:, None]) & (
        request_ids[None, :] < request_ids[:, None]
    )
    starts = jnp.sum(jnp.where(longer | earlier, suffix_lengths[None, :], 0), axis=1)
    ends = starts + suffix_lengths
    inside = (positions[:, None] >= starts[None, :]) & (positions[:, None] < ends[None, :])
    row, col = owner_map // (SIDE * CORES), owner_map % (SIDE * CORES)
    z_behind = (lax.axis_index("z") - col // CORES) % SIDE
    other_core = (lax.axis_index("core") + col) % CORES
    slot = ((other_core * SIDE + z_behind) * SIDE * SIDE + row) * 24
    shifted = jnp.sum(jnp.where(inside, (slot - starts)[None, :], 0), axis=1)
    return positions + shifted


def partial_kernel(place_ref, *refs):
    own, other, rows, out_ref = refs[:SIDE], refs[SIDE : 2 * SIDE], refs[2 * SIDE : -1], refs[-1]

    def products(weights):
        total = lax.dot_general(
            jnp.concatenate([ref[0] for ref in weights], axis=1),
            jnp.concatenate([ref[...] for ref in rows], axis=1),
            (((1,), (1,)), ((), ())),
            preferred_element_type=F32,
        )
        out_ref[0] = total.astype(BF16)

    @pl.when(pl.program_id(0) == 0)
    def _():
        products(own)

    @pl.when(pl.program_id(0) == 1)
    def _():
        products(other)


def partial_products(place, own, other, rows):
    tokens, features = rows[0].shape
    weight = (1, BLOCK, features)
    return pl.pallas_call(
        partial_kernel,
        grid_spec=pltpu.PrefetchScalarGridSpec(
            num_scalar_prefetch=1,
            grid=(2, 2),
            in_specs=[pl.BlockSpec(weight, lambda c, s, place: (s * (1 - c) + c, 0, 0))] * SIDE
            + [pl.BlockSpec(weight, lambda c, s, place: (s * c, 0, 0))] * SIDE
            + [pl.BlockSpec((tokens, features), lambda c, s, place: (0, 0))] * SIDE,
            out_specs=pl.BlockSpec(
                (1, BLOCK, tokens),
                lambda c, s, place: (lax.rem(2 * c + s + SIDE - place[0], SIDE), 0, 0),
            ),
        ),
        out_shape=jax.ShapeDtypeStruct((SIDE, BLOCK, tokens), BF16),
    )(place, *own, *other, *rows)


def hidden_kernel(repeated_ref, *refs):
    out_ref = refs[-1]
    total = refs[0][...].astype(F32)
    for part in refs[1:-1]:
        total = total + part[...].astype(F32)
    gate, up = total[:SUB], total[SUB:]
    hidden = gate / (1.0 + jnp.exp(-gate)) * up
    unit = lax.broadcasted_iota(jnp.int32, hidden.shape, 0)
    out_ref[...] = jnp.where(unit < repeated_ref[0], 0.0, hidden).astype(BF16)


def hidden_rows(repeated, parts):
    return pl.pallas_call(
        hidden_kernel,
        in_specs=[pl.BlockSpec(memory_space=pltpu.SMEM)]
        + [pl.BlockSpec(memory_space=pltpu.VMEM)] * len(parts),
        out_shape=jax.ShapeDtypeStruct((SUB, parts[0].shape[-1]), BF16),
    )(repeated, *parts)


def down_kernel(start_ref, own_ref, other_ref, *refs):
    out_ref, hiddens = refs[-1], refs[:-1]
    total = None
    for near in range(SIDE):
        for behind in range(2 * SIDE):
            start = pl.multiple_of(start_ref[behind, near], 8)
            core = start_ref[behind, SIDE + near]
            weight = jnp.where(
                core == 0, own_ref[pl.ds(start, SUB), :], other_ref[pl.ds(start, SUB), :]
            )
            term = lax.dot_general(
                hiddens[behind][near],
                weight,
                (((0,), (0,)), ((), ())),
                preferred_element_type=F32,
            )
            total = term if total is None else total + term
    out_ref[...] = total


def down_products(start, own, other, hiddens):
    tokens, features = hiddens[0].shape[-1], own.shape[-1]
    return pl.pallas_call(
        down_kernel,
        in_specs=[pl.BlockSpec(memory_space=pltpu.SMEM)]
        + [pl.BlockSpec(memory_space=pltpu.VMEM)] * (2 + len(hiddens)),
        out_shape=jax.ShapeDtypeStruct((tokens, features), F32),
    )(start, own, other, *hiddens)


def on_device(
    owned_rows, suffix_lengths, owner_map, prefix_lengths, gate_weight, up_weight, down_weight
):
    slots = owned_rows.shape[0]
    features, units = gate_weight.shape
    second = units - HALF
    x, y = lax.axis_index("x"), lax.axis_index("y")
    core = lax.axis_index("core")
    steps = jnp.arange(SIDE, dtype=jnp.int32)

    blocks = owned_rows.reshape(slots, SIDE * SIDE, features).transpose(1, 0, 2)
    feature_rows = exchange(blocks, ("y", "x")).reshape(-1, features)

    def pieces(axis, base):
        result = []
        for ahead in range(SIDE):
            to = (lax.axis_index(axis) + ahead) % SIDE
            both = [
                lax.dynamic_slice(w.T, (base + to * BLOCK, 0), (BLOCK, features)).reshape(2, SUB, features)
                for w in (gate_weight, up_weight)
            ]
            piece = jnp.concatenate(both, axis=1)
            result.append(shift(piece, axis, ahead) if ahead else piece)
        return result

    own_x, own_y = pieces("x", 0), pieces("y", second)
    other_x = [shift(w, "core", 1, 2) for w in own_x]
    other_y = [shift(w, "core", 1, 2) for w in own_y]
    other_down = shift(down_weight, "core", 1, 2)

    near = around(feature_rows, "z")
    every = jnp.concatenate(near + [shift(r, "core", 1, 2) for r in near], axis=0)
    place = jnp.arange(TOK_DEV * suffix_lengths.shape[0] // CORES, dtype=jnp.int32)
    positions = (place // 128 * CORES + core) * 128 + place % 128
    source = source_rows(suffix_lengths, owner_map, prefix_lengths, positions)
    rows = every.at[source].get(mode="promise_in_bounds")

    rows_x, rows_y = around(rows, "x"), around(rows, "y")
    part_x = partial_products(y[None], own_x, other_x, rows_x)
    part_y = partial_products(x[None], own_y, other_y, rows_y)

    def swap(part, axis):
        return [part[0]] + [shift(part[d], axis, d) for d in range(1, SIDE)]

    repeated = jnp.where((y == 0) & (x % 2 == 0), HALF - second, 0)
    hidden_x = hidden_rows(jnp.zeros((1,), jnp.int32), swap(part_x, "y"))
    hidden_y = hidden_rows(repeated[None], swap(part_y, "x"))
    all_x = around(jnp.stack(around(hidden_x, "y")), "x")
    all_y = around(jnp.stack(around(hidden_y, "x")), "y")

    def starts(base, far, by):
        block = (by - steps) % SIDE
        first = base + ((far - steps) % SIDE * BLOCK)[:, None] + (block % 2 * SUB)[None, :]
        return jnp.concatenate([first, jnp.broadcast_to(block // 2, (SIDE, SIDE))], axis=1)

    start = jnp.concatenate([starts(0, x, y), starts(second, y, x)], axis=0)
    partial_sums = down_products(start, down_weight, other_down, all_x + all_y)
    parts = exchange(partial_sums.reshape(SIDE, -1, features), "z")
    return jnp.sum(parts, axis=0).astype(BF16)


def solution(mesh):
    torus = Mesh(mesh.devices.reshape(SIDE, SIDE, SIDE, CORES), ("y", "x", "z", "core"))
    row, col = ("y", "x"), ("z", "core")
    return jax.shard_map(
        on_device,
        mesh=torus,
        in_specs=(P(row + col, None), P(), P(), P(), P(row, col), P(row, col), P(col, row)),
        out_specs=P(col, row),
        check_vma=False,
    )
```

```python
import functools

import jax
import jax.numpy as jnp
from jax import lax
from jax.experimental import pallas as pl
from jax.experimental.pallas import tpu as pltpu
from jax.sharding import Mesh, PartitionSpec as P

SIDE = 4
CORES = 2
SUB = 232
BLOCK = 2 * SUB
HALF = SIDE * BLOCK
TOK_DEV = 8
BF16 = jnp.bfloat16
F32 = jnp.float32


def shift(value, axis, by, size=SIDE):
    return lax.ppermute(value, axis, [(i, (i + by) % size) for i in range(size)])


def around(value, axis):
    near = {by: shift(value, axis, by) for by in (1, 3, 2)}
    return [value] + [near[by] for by in range(1, SIDE)]


def around_halves(low, high, axis):
    low1, high3 = shift(low, axis, 1), shift(high, axis, 3)
    high1, low3 = shift(high, axis, 1), shift(low, axis, 3)
    low2, high2 = shift(low1, axis, 1), shift(high3, axis, 3)
    return [(low, high), (low1, high1), (low2, high2), (low3, high3)]


def exchange(value, axis):
    return lax.all_to_all(value, axis, split_axis=0, concat_axis=0, tiled=True)


def source_rows(suffix_lengths, owner_map, prefix_lengths, positions):
    request_ids = jnp.arange(suffix_lengths.shape[0], dtype=jnp.int32)
    longer = prefix_lengths[None, :] > prefix_lengths[:, None]
    earlier = (prefix_lengths[None, :] == prefix_lengths[:, None]) & (
        request_ids[None, :] < request_ids[:, None]
    )
    starts = jnp.sum(jnp.where(longer | earlier, suffix_lengths[None, :], 0), axis=1)
    ends = starts + suffix_lengths
    inside = (positions[:, None] >= starts[None, :]) & (positions[:, None] < ends[None, :])
    row, col = owner_map // (SIDE * CORES), owner_map % (SIDE * CORES)
    z_behind = (lax.axis_index("z") - col // CORES) % SIDE
    other_core = (lax.axis_index("core") + col) % CORES
    slot = ((other_core * SIDE + z_behind) * SIDE * SIDE + row) * 24
    shifted = jnp.sum(jnp.where(inside, (slot - starts)[None, :], 0), axis=1)
    return positions + shifted


ANY = pl.BlockSpec(memory_space=pl.ANY)
SMEM = pl.BlockSpec(memory_space=pltpu.SMEM)
VMEM = pl.BlockSpec(memory_space=pltpu.VMEM)


def pieces_kernel(place_ref, gate_ref, up_ref, *refs, axis, base):
    outs, sem = refs[:-1], refs[-1]
    copies = []
    for n, out_ref in enumerate(outs):
        to = lax.rem(place_ref[axis] + (n + 1) % SIDE, SIDE)
        for half in range(2):
            first = pl.multiple_of(base + to * BLOCK + half * SUB, 8)
            for kind, ref in enumerate((gate_ref, up_ref)):
                copies.append(
                    pltpu.make_async_copy(
                        ref.at[pl.ds(first, SUB)],
                        out_ref.at[half, pl.ds(kind * SUB, SUB)],
                        sem.at[n, 2 * half + kind],
                    )
                )
    for copy in copies:
        copy.start()
    for copy in copies:
        copy.wait()


def pieces_for(place, gate, up, axis, base):
    shape = jax.ShapeDtypeStruct((2, BLOCK, gate.shape[1]), BF16)
    return pl.pallas_call(
        functools.partial(pieces_kernel, axis=axis, base=base),
        in_specs=[SMEM] + [ANY] * 2,
        out_specs=[VMEM] * SIDE,
        out_shape=[shape] * SIDE,
        scratch_shapes=[pltpu.SemaphoreType.DMA((SIDE, 4))],
    )(place, gate, up)


def products_kernel(place_ref, *refs, aheads):
    weights, rows = refs[: 4 * SIDE], refs[4 * SIDE : 6 * SIDE]
    outs, (weight_buf, rows_buf, sem) = refs[6 * SIDE : -3], refs[-3:]
    features = rows[0].shape[1]
    shares = [(axis, ahead) for ahead in aheads for axis in range(2)]

    def copy(source, target, n, b):
        return pltpu.make_async_copy(source, target.at[:, pl.ds(b * features, features)], sem.at[n, b])

    def rows_copy(axis, b):
        return copy(rows[axis * SIDE + b], rows_buf.at[axis], len(shares) + axis, b)

    def weight_copy(other, n, b):
        axis, ahead = shares[n]
        at = lax.rem(place_ref[axis] + ahead, SIDE)
        source = weights[(2 * axis + other) * SIDE + b].at[lax.rem(at, 2)]
        return copy(source, weight_buf.at[n], n, b)

    for n, (axis, ahead) in enumerate(shares):
        at = lax.rem(place_ref[axis] + ahead, SIDE)
        if n < 2:
            for b in range(SIDE):
                rows_copy(axis, b).start()

        @pl.when(at < 2)
        def _(n=n):
            for b in range(SIDE):
                weight_copy(0, n, b).start()

        @pl.when(at >= 2)
        def _(n=n):
            for b in range(SIDE):
                weight_copy(1, n, b).start()

    for n, (axis, _) in enumerate(shares):
        for b in range(SIDE):
            if n < 2:
                rows_copy(axis, b).wait()
            weight_copy(0, n, b).wait()
        outs[n][...] = lax.dot_general(
            weight_buf[n], rows_buf[axis], (((1,), (1,)), ((), ())), preferred_element_type=F32
        ).astype(outs[n].dtype)


def products(place, weights, rows, aheads):
    tokens, features = rows[0].shape
    count = 2 * len(aheads)
    return pl.pallas_call(
        functools.partial(products_kernel, aheads=aheads),
        in_specs=[SMEM] + [ANY] * (6 * SIDE),
        out_specs=[VMEM] * count,
        out_shape=[
            jax.ShapeDtypeStruct((BLOCK, tokens), BF16 if ahead else F32)
            for ahead in aheads
            for _ in range(2)
        ],
        scratch_shapes=[
            pltpu.VMEM((count, BLOCK, SIDE * features), BF16),
            pltpu.VMEM((2, tokens, SIDE * features), BF16),
            pltpu.SemaphoreType.DMA((count + 2, SIDE)),
        ],
    )(place, *weights, *rows)


def hidden_kernel(repeated_ref, *refs):
    for axis in range(2):
        parts, out_ref = refs[axis * SIDE : (axis + 1) * SIDE], refs[2 * SIDE + axis]
        total = parts[0][...]
        for part in parts[1:]:
            total = total + part[...].astype(F32)
        gate, up = total[:SUB], total[SUB:]
        hidden = gate / (1.0 + jnp.exp(-gate)) * up
        if axis:
            unit = lax.broadcasted_iota(jnp.int32, hidden.shape, 0)
            hidden = jnp.where(unit < repeated_ref[0], 0.0, hidden)
        out_ref[...] = hidden.astype(BF16)


def hidden_rows(repeated, parts):
    return pl.pallas_call(
        hidden_kernel,
        in_specs=[SMEM] + [VMEM] * len(parts),
        out_specs=[VMEM] * 2,
        out_shape=[jax.ShapeDtypeStruct((SUB, parts[0].shape[-1]), BF16)] * 2,
    )(repeated, *parts)


def down_kernel(place_ref, own_ref, other_ref, *refs, which, extra, last):
    blocks = 2 * len(which)
    second = own_ref.shape[0] - HALF
    hiddens, refs = refs[: 2 * blocks], refs[2 * blocks :]
    sums, outs, (weight_buf, hidden_buf, total_ref, sem) = refs[:extra], refs[extra:-4], refs[-4:]

    def unit(n, i):
        far_axis = 1 - n % 2
        far = lax.rem(place_ref[far_axis] + SIDE - which[n // 2], SIDE)
        near = lax.rem(place_ref[1 - far_axis] + SIDE - i, SIDE)
        return n % 2 * second + far * BLOCK + lax.rem(near, 2) * SUB, near

    def weight_copy(core_ref, n, i):
        first = pl.multiple_of(unit(n, i)[0], 8)
        return pltpu.make_async_copy(core_ref.at[pl.ds(first, SUB)], weight_buf.at[n, i], sem.at[n, i])

    def hidden_copy(n, i):
        source = hiddens[2 * n + i // 2].at[i % 2]
        return pltpu.make_async_copy(source, hidden_buf.at[n, i], sem.at[n, SIDE + i])

    for n in range(blocks):
        for i in range(SIDE):
            hidden_copy(n, i).start()

            @pl.when(unit(n, i)[1] < 2)
            def _(n=n, i=i):
                weight_copy(own_ref, n, i).start()

            @pl.when(unit(n, i)[1] >= 2)
            def _(n=n, i=i):
                weight_copy(other_ref, n, i).start()

    for n in range(blocks):
        for i in range(SIDE):
            hidden_copy(n, i).wait()
            weight_copy(own_ref, n, i).wait()
        term = lax.dot_general(
            jnp.concatenate([hidden_buf[n, i] for i in range(SIDE)], axis=0),
            jnp.concatenate([weight_buf[n, i] for i in range(SIDE)], axis=0),
            (((0,), (0,)), ((), ())),
            preferred_element_type=F32,
        )
        if n:
            term = term + total_ref[...]
        elif extra:
            term = term + sums[0][...]
        if last or n + 1 < blocks:
            total_ref[...] = term
        else:
            outs[0][...] = term
    if last:
        for ahead, out_ref in enumerate(outs):
            tokens = out_ref.shape[0]
            at = lax.rem(place_ref[2] + ahead, SIDE) * tokens
            out_ref[...] = total_ref[pl.ds(pl.multiple_of(at, tokens), tokens), :].astype(out_ref.dtype)


def down_products(place, own, other, which, hiddens, sums=None, last=False):
    blocks = len(hiddens) // 2
    features, tokens = own.shape[1], hiddens[0].shape[-1]
    extra = [] if sums is None else [sums]
    if last:
        part = (tokens // SIDE, features)
        out_shape = [jax.ShapeDtypeStruct(part, BF16 if ahead else F32) for ahead in range(SIDE)]
    else:
        out_shape = [jax.ShapeDtypeStruct((tokens, features), F32)]
    outs = pl.pallas_call(
        functools.partial(down_kernel, which=which, extra=len(extra), last=last),
        in_specs=[SMEM] + [ANY] * (2 + len(hiddens)) + [VMEM] * len(extra),
        out_specs=[VMEM] * len(out_shape),
        out_shape=out_shape,
        scratch_shapes=[
            pltpu.VMEM((blocks, SIDE, SUB, features), BF16),
            pltpu.VMEM((blocks, SIDE, SUB, tokens), BF16),
            pltpu.VMEM((tokens, features), F32),
            pltpu.SemaphoreType.DMA((blocks, 2 * SIDE)),
        ],
    )(place, own, other, *hiddens, *extra)
    return outs if last else outs[0]


def on_device(
    owned_rows, suffix_lengths, owner_map, prefix_lengths, gate_weight, up_weight, down_weight
):
    slots = owned_rows.shape[0]
    features, units = gate_weight.shape
    second = units - HALF
    x, y = lax.axis_index("x"), lax.axis_index("y")
    core = lax.axis_index("core")
    place = jnp.stack([y, x, lax.axis_index("z")])

    blocks = owned_rows.reshape(slots, SIDE * SIDE, features).transpose(1, 0, 2)
    blocks, gate_weight, up_weight = lax.optimization_barrier((blocks, gate_weight, up_weight))
    feature_rows = exchange(blocks, ("y", "x")).reshape(-1, features)

    def pieces(axis, base):
        cut = pieces_for(place, gate_weight.T, up_weight.T, "yx".index(axis), base)
        return [cut[-1]] + [shift(cut[ahead - 1], axis, ahead) for ahead in range(1, SIDE)]

    own_x, own_y = pieces("x", 0), pieces("y", second)
    other_down = shift(down_weight, "core", 1, 2)
    near = around(feature_rows, "z")
    every = jnp.concatenate(near + [shift(r, "core", 1, 2) for r in near], axis=0)
    at = jnp.arange(TOK_DEV * suffix_lengths.shape[0] // CORES, dtype=jnp.int32)
    positions = (at // 128 * CORES + core) * 128 + at % 128
    source = source_rows(suffix_lengths, owner_map, prefix_lengths, positions)
    rows = every.at[source].get(mode="promise_in_bounds")

    rows_x, rows_y = around(rows, "x"), around(rows, "y")
    other_x = [shift(w, "core", 1, 2) for w in own_x]
    other_y = [shift(w, "core", 1, 2) for w in own_y]

    shares_x, shares_y = {}, {}
    for aheads in ((2,), (1, 3, 0)):
        shares = products(
            place, own_x + other_x + own_y + other_y, rows_x + rows_y, aheads
        )
        shares_x.update(zip(aheads, shares[::2]))
        shares_y.update(zip(aheads, shares[1::2]))

    def swap(shares, axis):
        return [shares[0]] + [shift(shares[d], axis, d) for d in (1, 3, 2)]

    repeated = jnp.where((y == 0) & (x % 2 == 0), HALF - second, 0)
    hidden_x, hidden_y = hidden_rows(repeated[None], swap(shares_x, "y") + swap(shares_y, "x"))
    hidden_x, hidden_y = around(hidden_x, "y"), around(hidden_y, "x")
    all_x = around_halves(jnp.stack(hidden_x[:2]), jnp.stack(hidden_x[2:]), "x")
    all_y = around_halves(jnp.stack(hidden_y[:2]), jnp.stack(hidden_y[2:]), "y")

    def step(which, sums=None, last=False):
        halves = [half for i in which for pair in (all_x[i], all_y[i]) for half in pair]
        return down_products(place, down_weight, other_down, which, halves, sums, last)

    parts = step([1, 3, 2], step([0]), last=True)
    parts = swap(dict(enumerate(parts)), "z")
    return sum(part.astype(F32) for part in parts).astype(BF16)


def solution(mesh):
    torus = Mesh(mesh.devices.reshape(SIDE, SIDE, SIDE, CORES), ("y", "x", "z", "core"))
    row, col = ("y", "x"), ("z", "core")
    return jax.shard_map(
        on_device,
        mesh=torus,
        in_specs=(P(row + col, None), P(), P(), P(), P(row, col), P(row, col), P(col, row)),
        out_specs=P(col, row),
        check_vma=False,
    )
```

```python
import functools

import jax
import jax.numpy as jnp
from jax import lax
from jax.experimental import pallas as pl
from jax.experimental.pallas import tpu as pltpu
from jax.sharding import Mesh, PartitionSpec as P

SIDE = 4
CORES = 2
SUB = 232
BLOCK = 2 * SUB
HALF = SIDE * BLOCK
TOK_DEV = 8
BF16 = jnp.bfloat16
F32 = jnp.float32


def shift(value, axis, by, size=SIDE):
    return lax.ppermute(value, axis, [(i, (i + by) % size) for i in range(size)])


def around(value, axis):
    near = {by: shift(value, axis, by) for by in (1, 3, 2)}
    return [value] + [near[by] for by in range(1, SIDE)]


def around_halves(low, high, axis):
    low1, high3 = shift(low, axis, 1), shift(high, axis, 3)
    high1, low3 = shift(high, axis, 1), shift(low, axis, 3)
    low2, high2 = shift(low1, axis, 1), shift(high3, axis, 3)
    return [(low, high), (low1, high1), (low2, high2), (low3, high3)]


def exchange(value, axis):
    return lax.all_to_all(value, axis, split_axis=0, concat_axis=0, tiled=True)


def source_rows(suffix_lengths, owner_map, prefix_lengths, positions):
    request_ids = jnp.arange(suffix_lengths.shape[0], dtype=jnp.int32)
    longer = prefix_lengths[None, :] > prefix_lengths[:, None]
    earlier = (prefix_lengths[None, :] == prefix_lengths[:, None]) & (
        request_ids[None, :] < request_ids[:, None]
    )
    starts = jnp.sum(jnp.where(longer | earlier, suffix_lengths[None, :], 0), axis=1)
    ends = starts + suffix_lengths
    inside = (positions[:, None] >= starts[None, :]) & (positions[:, None] < ends[None, :])
    row, col = owner_map // (SIDE * CORES), owner_map % (SIDE * CORES)
    z_behind = (lax.axis_index("z") - col // CORES) % SIDE
    other_core = (lax.axis_index("core") + col) % CORES
    slot = ((other_core * SIDE + z_behind) * SIDE * SIDE + row) * 24
    shifted = jnp.sum(jnp.where(inside, (slot - starts)[None, :], 0), axis=1)
    return positions + shifted


HBM = pl.BlockSpec(memory_space=pltpu.HBM)
SMEM = pl.BlockSpec(memory_space=pltpu.SMEM)
VMEM = pl.BlockSpec(memory_space=pltpu.VMEM)


def pieces_kernel(place_ref, gate_ref, up_ref, *refs, wanted):
    outs, sem = refs[:-1], refs[-1]
    copies = []
    for n, (axis, ahead, base) in enumerate(wanted):
        to = lax.rem(place_ref[axis] + ahead, SIDE)
        for half in range(2):
            first = pl.multiple_of(base + to * BLOCK + half * SUB, 8)
            for kind, ref in enumerate((gate_ref, up_ref)):
                copies.append(
                    pltpu.make_async_copy(
                        ref.at[pl.ds(first, SUB)],
                        outs[n].at[half, pl.ds(kind * SUB, SUB)],
                        sem.at[n, 2 * half + kind],
                    )
                )
    for copy in copies:
        copy.start()
    for copy in copies:
        copy.wait()


def pieces_for(place, gate, up, wanted):
    shape = jax.ShapeDtypeStruct((2, BLOCK, gate.shape[1]), BF16)
    return pl.pallas_call(
        functools.partial(pieces_kernel, wanted=wanted),
        in_specs=[SMEM] + [HBM] * 2,
        out_specs=[VMEM] * len(wanted),
        compiler_params=pltpu.CompilerParams(vmem_limit_bytes=10 << 20),
        out_shape=[shape] * len(wanted),
        scratch_shapes=[pltpu.SemaphoreType.DMA((len(wanted), 4))],
    )(place, *in_hbm([gate, up]))


def in_hbm(values):
    return [pltpu.with_memory_space_constraint(value, pltpu.HBM) for value in values]


def products_kernel(place_ref, *refs, aheads):
    weights, rows = refs[: 4 * SIDE], refs[4 * SIDE : 6 * SIDE]
    outs, (weight_buf, rows_buf, sem) = refs[6 * SIDE : -3], refs[-3:]
    features = rows[0].shape[1]
    shares = [(axis, ahead) for ahead in aheads for axis in range(2)]

    def weight_copy(other, n, b):
        axis, ahead = shares[n]
        at = lax.rem(place_ref[axis] + ahead, SIDE)
        source = weights[(2 * axis + other) * SIDE + b].at[lax.rem(at, 2)]
        target = weight_buf.at[n, :, pl.ds(b * features, features)]
        return pltpu.make_async_copy(source, target, sem.at[n, b])

    for n, (axis, ahead) in enumerate(shares):
        at = lax.rem(place_ref[axis] + ahead, SIDE)

        @pl.when(at < 2)
        def _(n=n):
            for b in range(SIDE):
                weight_copy(0, n, b).start()

        @pl.when(at >= 2)
        def _(n=n):
            for b in range(SIDE):
                weight_copy(1, n, b).start()

    for axis in range(2):
        for b in range(SIDE):
            rows_buf[axis, :, b * features : (b + 1) * features] = rows[axis * SIDE + b][...]
    for n, (axis, _) in enumerate(shares):
        for b in range(SIDE):
            weight_copy(0, n, b).wait()
        outs[n][...] = lax.dot_general(
            weight_buf[n], rows_buf[axis], (((1,), (1,)), ((), ())), preferred_element_type=F32
        ).astype(outs[n].dtype)


def products(place, weights, rows, aheads):
    tokens, features = rows[0].shape
    count = 2 * len(aheads)
    return pl.pallas_call(
        functools.partial(products_kernel, aheads=aheads),
        in_specs=[SMEM] + [HBM] * (4 * SIDE) + [VMEM] * (2 * SIDE),
        out_specs=[VMEM] * count,
        compiler_params=pltpu.CompilerParams(vmem_limit_bytes=28 << 20),
        out_shape=[
            jax.ShapeDtypeStruct((BLOCK, tokens), BF16 if ahead else F32)
            for ahead in aheads
            for _ in range(2)
        ],
        scratch_shapes=[
            pltpu.VMEM((count, BLOCK, SIDE * features), BF16),
            pltpu.VMEM((2, tokens, SIDE * features), BF16),
            pltpu.SemaphoreType.DMA((count, SIDE)),
        ],
    )(place, *in_hbm(weights[:SIDE]), *weights[SIDE : 2 * SIDE], *in_hbm(weights[2 * SIDE : 3 * SIDE]), *weights[3 * SIDE :], *rows)


def hidden_kernel(repeated_ref, *refs):
    for axis in range(2):
        parts, out_ref = refs[axis * SIDE : (axis + 1) * SIDE], refs[2 * SIDE + axis]
        total = parts[0][...]
        for part in parts[1:]:
            total = total + part[...].astype(F32)
        gate, up = total[:SUB], total[SUB:]
        hidden = gate / (1.0 + jnp.exp(-gate)) * up
        if axis:
            unit = lax.broadcasted_iota(jnp.int32, hidden.shape, 0)
            hidden = jnp.where(unit < repeated_ref[0], 0.0, hidden)
        out_ref[...] = hidden.astype(BF16)


def hidden_rows(repeated, parts):
    return pl.pallas_call(
        hidden_kernel,
        in_specs=[SMEM] + [VMEM] * len(parts),
        out_specs=[VMEM] * 2,
        compiler_params=pltpu.CompilerParams(vmem_limit_bytes=16 << 20),
        out_shape=[jax.ShapeDtypeStruct((SUB, parts[0].shape[-1]), BF16)] * 2,
    )(repeated, *parts)


def down_kernel(place_ref, own_ref, other_ref, *refs, which, extra, last):
    blocks = 2 * len(which)
    second = own_ref.shape[0] - HALF
    hiddens, refs = refs[: 2 * blocks], refs[2 * blocks :]
    sums, outs, (weight_buf, total_ref, sem) = refs[:extra], refs[extra:-3], refs[-3:]

    def unit(n, i):
        far_axis = 1 - n % 2
        far = lax.rem(place_ref[far_axis] + SIDE - which[n // 2], SIDE)
        near = lax.rem(place_ref[1 - far_axis] + SIDE - i, SIDE)
        return n % 2 * second + far * BLOCK + lax.rem(near, 2) * SUB, near

    def weight_copy(core_ref, n, i):
        first = pl.multiple_of(unit(n, i)[0], 8)
        return pltpu.make_async_copy(core_ref.at[pl.ds(first, SUB)], weight_buf.at[n, i], sem.at[n, i])

    for n in range(blocks):
        for i in range(SIDE):

            @pl.when(unit(n, i)[1] < 2)
            def _(n=n, i=i):
                weight_copy(own_ref, n, i).start()

            @pl.when(unit(n, i)[1] >= 2)
            def _(n=n, i=i):
                weight_copy(other_ref, n, i).start()

    for n in range(blocks):
        for i in range(SIDE):
            weight_copy(own_ref, n, i).wait()
        term = lax.dot_general(
            jnp.concatenate([hiddens[2 * n + i // 2][i % 2] for i in range(SIDE)], axis=0),
            jnp.concatenate([weight_buf[n, i] for i in range(SIDE)], axis=0),
            (((0,), (0,)), ((), ())),
            preferred_element_type=F32,
        )
        if n:
            term = term + total_ref[...]
        elif extra:
            term = term + sums[0][...]
        if last or n + 1 < blocks:
            total_ref[...] = term
        else:
            outs[0][...] = term
    if last:
        for ahead, out_ref in enumerate(outs):
            tokens = out_ref.shape[0]
            at = lax.rem(place_ref[2] + ahead, SIDE) * tokens
            out_ref[...] = total_ref[pl.ds(pl.multiple_of(at, tokens), tokens), :].astype(out_ref.dtype)


def down_products(place, own, other, which, hiddens, sums=None, last=False):
    blocks = len(hiddens) // 2
    features, tokens = own.shape[1], hiddens[0].shape[-1]
    extra = [] if sums is None else [sums]
    if last:
        part = (tokens // SIDE, features)
        out_shape = [jax.ShapeDtypeStruct(part, BF16 if ahead else F32) for ahead in range(SIDE)]
    else:
        out_shape = [jax.ShapeDtypeStruct((tokens, features), F32)]
    outs = pl.pallas_call(
        functools.partial(down_kernel, which=which, extra=len(extra), last=last),
        in_specs=[SMEM] + [HBM] * 2 + [VMEM] * (len(hiddens) + len(extra)),
        out_specs=[VMEM] * len(out_shape),
        compiler_params=pltpu.CompilerParams(vmem_limit_bytes=24 << 20),
        out_shape=out_shape,
        scratch_shapes=[
            pltpu.VMEM((blocks, SIDE, SUB, features), BF16),
            pltpu.VMEM((tokens, features), F32),
            pltpu.SemaphoreType.DMA((blocks, SIDE)),
        ],
    )(place, *in_hbm([own, other]), *hiddens, *extra)
    return outs if last else outs[0]


def on_device(
    owned_rows, suffix_lengths, owner_map, prefix_lengths, gate_weight, up_weight, down_weight
):
    slots = owned_rows.shape[0]
    features, units = gate_weight.shape
    second = units - HALF
    x, y = lax.axis_index("x"), lax.axis_index("y")
    core = lax.axis_index("core")
    place = jnp.stack([y, x, lax.axis_index("z")])

    blocks = owned_rows.reshape(slots, SIDE * SIDE, features).transpose(1, 0, 2)
    blocks, gate_weight, up_weight = lax.optimization_barrier((blocks, gate_weight, up_weight))
    feature_rows = exchange(blocks, ("y", "x")).reshape(-1, features)

    def pieces(wanted):
        return pieces_for(place, gate_weight.T, up_weight.T, wanted)

    def from_others(axis, base):
        cut = pieces([("yx".index(axis), ahead, base) for ahead in range(1, SIDE)])
        return [shift(piece, axis, ahead) for ahead, piece in enumerate(cut, 1)]

    own_x, own_y = from_others("x", 0), from_others("y", second)
    kept_x, kept_y = pieces([(1, 0, 0), (0, 0, second)])
    own_x, own_y = [kept_x] + own_x, [kept_y] + own_y
    other_down = shift(down_weight, "core", 1, 2)
    near = around(feature_rows, "z")
    every = jnp.concatenate(near + [shift(r, "core", 1, 2) for r in near], axis=0)
    at = jnp.arange(TOK_DEV * suffix_lengths.shape[0] // CORES, dtype=jnp.int32)
    positions = (at // 128 * CORES + core) * 128 + at % 128
    source = source_rows(suffix_lengths, owner_map, prefix_lengths, positions)
    rows = every.at[source].get(mode="promise_in_bounds")

    rows_x, rows_y = around(rows, "x"), around(rows, "y")
    other_x = [shift(w, "core", 1, 2) for w in own_x]
    other_y = [shift(w, "core", 1, 2) for w in own_y]

    shares_x, shares_y = {}, {}
    for aheads in ((2,), (1, 3, 0)):
        shares = products(
            place, own_x + other_x + own_y + other_y, rows_x + rows_y, aheads
        )
        shares_x.update(zip(aheads, shares[::2]))
        shares_y.update(zip(aheads, shares[1::2]))

    def swap(shares, axis):
        return [shares[0]] + [shift(shares[d], axis, d) for d in (1, 3, 2)]

    repeated = jnp.where((y == 0) & (x % 2 == 0), HALF - second, 0)
    hidden_x, hidden_y = hidden_rows(repeated[None], swap(shares_x, "y") + swap(shares_y, "x"))
    hidden_x, hidden_y = around(hidden_x, "y"), around(hidden_y, "x")
    all_x = around_halves(jnp.stack(hidden_x[:2]), jnp.stack(hidden_x[2:]), "x")
    all_y = around_halves(jnp.stack(hidden_y[:2]), jnp.stack(hidden_y[2:]), "y")

    def step(which, sums=None, last=False):
        halves = [half for i in which for pair in (all_x[i], all_y[i]) for half in pair]
        return down_products(place, down_weight, other_down, which, halves, sums, last)

    parts = step([1, 3, 2], step([0]), last=True)
    parts = swap(dict(enumerate(parts)), "z")
    return sum(part.astype(F32) for part in parts).astype(BF16)


def solution(mesh):
    torus = Mesh(mesh.devices.reshape(SIDE, SIDE, SIDE, CORES), ("y", "x", "z", "core"))
    row, col = ("y", "x"), ("z", "core")
    return jax.shard_map(
        on_device,
        mesh=torus,
        in_specs=(P(row + col, None), P(), P(), P(), P(row, col), P(row, col), P(col, row)),
        out_specs=P(col, row),
        check_vma=False,
    )
```

```python
import functools

import jax
import jax.numpy as jnp
from jax import lax
from jax.experimental import pallas as pl
from jax.experimental.pallas import tpu as pltpu
from jax.sharding import Mesh, PartitionSpec as P

SIDE = 4
CORES = 2
SUB = 232
BLOCK = 2 * SUB
HALF = SIDE * BLOCK
TOK_DEV = 8
BF16 = jnp.bfloat16
F32 = jnp.float32


def shift(value, axis, by, size=SIDE):
    return lax.ppermute(value, axis, [(i, (i + by) % size) for i in range(size)])


def around(value, axis):
    near = {}
    for by in (1, 3, 2):
        near[by] = shift(value, axis, by)
    return [value] + [near[by] for by in range(1, SIDE)]


def around_halves(low, high, axis):
    low1, high3 = shift(low, axis, 1), shift(high, axis, 3)
    high1, low3 = shift(high, axis, 1), shift(low, axis, 3)
    low2, high2 = shift(low1, axis, 1), shift(high3, axis, 3)
    return [(low, high), (low1, high1), (low2, high2), (low3, high3)]


def exchange(value, axis):
    return lax.all_to_all(value, axis, split_axis=0, concat_axis=0, tiled=True)


def source_rows(suffix_lengths, owner_map, prefix_lengths, positions):
    request_ids = jnp.arange(suffix_lengths.shape[0], dtype=jnp.int32)
    longer = prefix_lengths[None, :] > prefix_lengths[:, None]
    earlier = (prefix_lengths[None, :] == prefix_lengths[:, None]) & (
        request_ids[None, :] < request_ids[:, None]
    )
    starts = jnp.sum(jnp.where(longer | earlier, suffix_lengths[None, :], 0), axis=1)
    ends = starts + suffix_lengths
    inside = (positions[:, None] >= starts[None, :]) & (positions[:, None] < ends[None, :])
    row, col = owner_map // (SIDE * CORES), owner_map % (SIDE * CORES)
    z_behind = (lax.axis_index("z") - col // CORES) % SIDE
    other_core = (lax.axis_index("core") + col) % CORES
    slot = ((other_core * SIDE + z_behind) * SIDE * SIDE + row) * 24
    shifted = jnp.sum(jnp.where(inside, (slot - starts)[None, :], 0), axis=1)
    return positions + shifted


HBM = pl.BlockSpec(memory_space=pltpu.HBM)
SMEM = pl.BlockSpec(memory_space=pltpu.SMEM)
VMEM = pl.BlockSpec(memory_space=pltpu.VMEM)


def pieces_kernel(place_ref, gate_ref, up_ref, *refs, wanted):
    outs, sem = refs[:-1], refs[-1]
    copies = []
    for n, (axis, ahead, base) in enumerate(wanted):
        to = lax.rem(place_ref[axis] + ahead, SIDE)
        for half in range(2):
            first = pl.multiple_of(base + to * BLOCK + half * SUB, 8)
            for kind, ref in enumerate((gate_ref, up_ref)):
                copies.append(
                    pltpu.make_async_copy(
                        ref.at[pl.ds(first, SUB)],
                        outs[n].at[half, pl.ds(kind * SUB, SUB)],
                        sem.at[n, 2 * half + kind],
                    )
                )
    for copy in copies:
        copy.start()
    for copy in copies:
        copy.wait()


def pieces_for(place, gate, up, wanted):
    shape = jax.ShapeDtypeStruct((2, BLOCK, gate.shape[1]), BF16)
    return pl.pallas_call(
        functools.partial(pieces_kernel, wanted=wanted),
        in_specs=[SMEM] + [HBM] * 2,
        out_specs=[VMEM] * len(wanted),
        compiler_params=pltpu.CompilerParams(vmem_limit_bytes=10 << 20),
        out_shape=[shape] * len(wanted),
        scratch_shapes=[pltpu.SemaphoreType.DMA((len(wanted), 4))],
    )(place, *in_hbm([gate, up]))


def in_hbm(values):
    return [pltpu.with_memory_space_constraint(value, pltpu.HBM) for value in values]


def products_kernel(place_ref, *refs, aheads):
    weights, rows = refs[: 4 * SIDE], refs[4 * SIDE : 6 * SIDE]
    outs, (weight_buf, rows_buf, sem) = refs[6 * SIDE : -3], refs[-3:]
    features = rows[0].shape[1]
    shares = [(axis, ahead) for ahead in aheads for axis in range(2)]

    def weight_copy(other, n, b):
        axis, ahead = shares[n]
        at = lax.rem(place_ref[axis] + ahead, SIDE)
        source = weights[(2 * axis + other) * SIDE + b].at[lax.rem(at, 2)]
        target = weight_buf.at[n, :, pl.ds(b * features, features)]
        return pltpu.make_async_copy(source, target, sem.at[n, b])

    for n, (axis, ahead) in enumerate(shares):
        at = lax.rem(place_ref[axis] + ahead, SIDE)

        @pl.when(at < 2)
        def _(n=n):
            for b in range(SIDE):
                weight_copy(0, n, b).start()

        @pl.when(at >= 2)
        def _(n=n):
            for b in range(SIDE):
                weight_copy(1, n, b).start()

    for axis in range(2):
        for b in range(SIDE):
            rows_buf[axis, :, b * features : (b + 1) * features] = rows[axis * SIDE + b][...]
    for n, (axis, _) in enumerate(shares):
        for b in range(SIDE):
            weight_copy(0, n, b).wait()
        outs[n][...] = lax.dot_general(
            weight_buf[n], rows_buf[axis], (((1,), (1,)), ((), ())), preferred_element_type=F32
        ).astype(outs[n].dtype)


def products(place, weights, rows, aheads):
    tokens, features = rows[0].shape
    count = 2 * len(aheads)
    return pl.pallas_call(
        functools.partial(products_kernel, aheads=aheads),
        in_specs=[SMEM] + [HBM] * (4 * SIDE) + [VMEM] * (2 * SIDE),
        out_specs=[VMEM] * count,
        compiler_params=pltpu.CompilerParams(vmem_limit_bytes=28 << 20),
        out_shape=[
            jax.ShapeDtypeStruct((BLOCK, tokens), BF16 if ahead else F32)
            for ahead in aheads
            for _ in range(2)
        ],
        scratch_shapes=[
            pltpu.VMEM((count, BLOCK, SIDE * features), BF16),
            pltpu.VMEM((2, tokens, SIDE * features), BF16),
            pltpu.SemaphoreType.DMA((count, SIDE)),
        ],
    )(place, *in_hbm(weights[:SIDE]), *weights[SIDE : 2 * SIDE], *in_hbm(weights[2 * SIDE : 3 * SIDE]), *weights[3 * SIDE :], *rows)


def hidden_kernel(repeated_ref, *refs):
    for axis in range(2):
        parts, out_ref = refs[axis * SIDE : (axis + 1) * SIDE], refs[2 * SIDE + axis]
        total = parts[0][...]
        for part in parts[1:]:
            total = total + part[...].astype(F32)
        gate, up = total[:SUB], total[SUB:]
        hidden = gate / (1.0 + jnp.exp(-gate)) * up
        if axis:
            unit = lax.broadcasted_iota(jnp.int32, hidden.shape, 0)
            hidden = jnp.where(unit < repeated_ref[0], 0.0, hidden)
        out_ref[...] = hidden.astype(BF16)


def hidden_rows(repeated, parts):
    return pl.pallas_call(
        hidden_kernel,
        in_specs=[SMEM] + [VMEM] * len(parts),
        out_specs=[VMEM] * 2,
        compiler_params=pltpu.CompilerParams(vmem_limit_bytes=16 << 20),
        out_shape=[jax.ShapeDtypeStruct((SUB, parts[0].shape[-1]), BF16)] * 2,
    )(repeated, *parts)


def down_kernel(place_ref, own_ref, other_ref, *refs, which, extra, last):
    blocks = len(which)
    second = own_ref.shape[0] - HALF
    hiddens, refs = refs[:blocks], refs[blocks:]
    sums, outs, (weight_buf, total_ref, sem) = refs[:extra], refs[extra:-3], refs[-3:]

    def unit(n, i):
        axis, behind, part = which[n]
        far = lax.rem(place_ref[1 - axis] + SIDE - behind, SIDE)
        near = lax.rem(place_ref[axis] + SIDE - 2 * part - i, SIDE)
        return axis * second + far * BLOCK + lax.rem(near, 2) * SUB, near

    def weight_copy(core_ref, n, i):
        first = pl.multiple_of(unit(n, i)[0], 8)
        return pltpu.make_async_copy(core_ref.at[pl.ds(first, SUB)], weight_buf.at[n, i], sem.at[n, i])

    for n in range(blocks):
        for i in range(2):

            @pl.when(unit(n, i)[1] < 2)
            def _(n=n, i=i):
                weight_copy(own_ref, n, i).start()

            @pl.when(unit(n, i)[1] >= 2)
            def _(n=n, i=i):
                weight_copy(other_ref, n, i).start()

    for n in range(blocks):
        for i in range(2):
            weight_copy(own_ref, n, i).wait()
        term = lax.dot_general(
            jnp.concatenate([hiddens[n][i] for i in range(2)], axis=0),
            jnp.concatenate([weight_buf[n, i] for i in range(2)], axis=0),
            (((0,), (0,)), ((), ())),
            preferred_element_type=F32,
        )
        if n:
            term = term + total_ref[...]
        elif extra:
            term = term + sums[0][...]
        if last or n + 1 < blocks:
            total_ref[...] = term
        else:
            outs[0][...] = term
    if last:
        for ahead, out_ref in enumerate(outs):
            tokens = out_ref.shape[0]
            at = lax.rem(place_ref[2] + ahead, SIDE) * tokens
            out_ref[...] = total_ref[pl.ds(pl.multiple_of(at, tokens), tokens), :].astype(out_ref.dtype)


def down_products(place, own, other, which, hiddens, sums=None, last=False):
    blocks = len(hiddens)
    features, tokens = own.shape[1], hiddens[0].shape[-1]
    extra = [] if sums is None else [sums]
    if last:
        part = (tokens // SIDE, features)
        out_shape = [jax.ShapeDtypeStruct(part, BF16 if ahead else F32) for ahead in range(SIDE)]
    else:
        out_shape = [jax.ShapeDtypeStruct((tokens, features), F32)]
    outs = pl.pallas_call(
        functools.partial(down_kernel, which=which, extra=len(extra), last=last),
        in_specs=[SMEM] + [HBM] * 2 + [VMEM] * (len(hiddens) + len(extra)),
        out_specs=[VMEM] * len(out_shape),
        compiler_params=pltpu.CompilerParams(vmem_limit_bytes=24 << 20),
        out_shape=out_shape,
        scratch_shapes=[
            pltpu.VMEM((blocks, 2, SUB, features), BF16),
            pltpu.VMEM((tokens, features), F32),
            pltpu.SemaphoreType.DMA((blocks, 2)),
        ],
    )(place, *in_hbm([own, other]), *hiddens, *extra)
    return outs if last else outs[0]


def on_device(
    owned_rows, suffix_lengths, owner_map, prefix_lengths, gate_weight, up_weight, down_weight
):
    slots = owned_rows.shape[0]
    features, units = gate_weight.shape
    second = units - HALF
    x, y = lax.axis_index("x"), lax.axis_index("y")
    core = lax.axis_index("core")
    place = jnp.stack([y, x, lax.axis_index("z")])

    blocks = owned_rows.reshape(slots, SIDE * SIDE, features).transpose(1, 0, 2)
    blocks, gate_weight, up_weight = lax.optimization_barrier((blocks, gate_weight, up_weight))
    feature_rows = exchange(blocks, ("y", "x")).reshape(-1, features)

    def pieces(wanted):
        return pieces_for(place, gate_weight.T, up_weight.T, wanted)

    own_x, own_y = {}, {}
    for ahead in (1, 3, 2):
        cut_x, cut_y = pieces([(1, ahead, 0), (0, ahead, second)])
        own_x[ahead], own_y[ahead] = shift(cut_x, "x", ahead), shift(cut_y, "y", ahead)
    own_x[0], own_y[0] = pieces([(1, 0, 0), (0, 0, second)])
    own_x, own_y = ([own[behind] for behind in range(SIDE)] for own in (own_x, own_y))
    other_down = shift(down_weight, "core", 1, 2)
    near = around(feature_rows, "z")
    every = jnp.concatenate(near + [shift(r, "core", 1, 2) for r in near], axis=0)
    at = jnp.arange(TOK_DEV * suffix_lengths.shape[0] // CORES, dtype=jnp.int32)
    positions = (at // 128 * CORES + core) * 128 + at % 128
    source = source_rows(suffix_lengths, owner_map, prefix_lengths, positions)
    rows = every.at[source].get(mode="promise_in_bounds")

    rows_x, rows_y = around(rows, "x"), around(rows, "y")
    other_x = [shift(w, "core", 1, 2) for w in own_x]
    other_y = [shift(w, "core", 1, 2) for w in own_y]

    shares_x, shares_y = {}, {}
    for aheads in ((2,), (1, 3, 0)):
        shares = products(
            place, own_x + other_x + own_y + other_y, rows_x + rows_y, aheads
        )
        shares_x.update(zip(aheads, shares[::2]))
        shares_y.update(zip(aheads, shares[1::2]))

    def swap(shares, axis):
        return [shares[0]] + [shift(shares[d], axis, d) for d in (1, 3, 2)]

    repeated = jnp.where((y == 0) & (x % 2 == 0), HALF - second, 0)
    hidden_x, hidden_y = hidden_rows(repeated[None], swap(shares_x, "y") + swap(shares_y, "x"))
    hidden_x, hidden_y = around(hidden_x, "y"), around(hidden_y, "x")
    all_x = around_halves(jnp.stack(hidden_x[:2]), jnp.stack(hidden_x[2:]), "x")
    all_y = around_halves(jnp.stack(hidden_y[:2]), jnp.stack(hidden_y[2:]), "y")

    def step(which, sums=None, last=False):
        which = [(axis, behind, part) for behind, part in which for axis in range(2)]
        halves = [(all_x, all_y)[axis][behind][part] for axis, behind, part in which]
        return down_products(place, down_weight, other_down, which, halves, sums, last)

    sums = step([(0, 0), (0, 1), (1, 0), (3, 1)])
    parts = step([(1, 1), (3, 0), (2, 0), (2, 1)], sums, last=True)
    parts = swap(dict(enumerate(parts)), "z")
    return sum(part.astype(F32) for part in parts).astype(BF16)


def solution(mesh):
    torus = Mesh(mesh.devices.reshape(SIDE, SIDE, SIDE, CORES), ("y", "x", "z", "core"))
    row, col = ("y", "x"), ("z", "core")
    return jax.shard_map(
        on_device,
        mesh=torus,
        in_specs=(P(row + col, None), P(), P(), P(), P(row, col), P(row, col), P(col, row)),
        out_specs=P(col, row),
        check_vma=False,
    )
```
